32 devices in a mesh: exp: 4 (over x, core), fsdp: 8 (over z, y).
Axes of the slice: x: 2, y: 2, z: 4, core: 2. Of those that a mesh axis runs over, the one named last changes fastest.
Arguments:
- tokens: bfloat16 [8192, 1536], P(('exp', 'fsdp')), may hold values from -6 to 6
- cotangent: bfloat16 [8192, 1536], P(('exp', 'fsdp')), may hold values from -6 to 6
- prefix: int32 [32], P(('exp', 'fsdp')), may hold values from 25 to 128
- routes: int32 [8192, 8], P(('exp', 'fsdp')), may hold values from 0 to 19, all different within a row; in each aligned block of 256 rows (0 to 255, 256 to 511, ...) at most 128 rows name the same one
- attention_gain: bfloat16 [1536], P('fsdp'), may hold values from 0.5 to 1.5
- expert_gain: bfloat16 [1536], P('fsdp'), may hold values from 0.5 to 1.5
- query_weight: bfloat16 [1536, 1536], P('fsdp'), may hold values from -0.21875 to 0.21875
- key_weight: bfloat16 [1536, 512], P('fsdp'), may hold values from -0.21875 to 0.21875
- value_weight: bfloat16 [1536, 512], P('fsdp'), may hold values from -0.15625 to 0.15625
- output_weight: bfloat16 [1536, 1536], P('fsdp'), may hold values from -1.796875 to 1.796875
- router_weight: bfloat16 [1536, 20], P('fsdp'), may hold values from -0.078125 to 0.078125
- gate_weight: bfloat16 [20, 1536, 512], P('exp', 'fsdp'), may hold values from -0.15625 to 0.15625
- up_weight: bfloat16 [20, 1536, 512], P('exp', 'fsdp'), may hold values from -0.15625 to 0.15625
- down_weight: bfloat16 [20, 512, 1536], P('exp', 'fsdp'), may hold values from -4.1875 to 4.1875
Outputs:
- block_out: bfloat16 [8192, 1536], P(('exp', 'fsdp'))
- input_grad: float32 [8192, 1536], P(('exp', 'fsdp'))
- attention_gain_grad: float32 [1536], P('fsdp')
- expert_gain_grad: float32 [1536], P('fsdp')
- query_weight_grad: float32 [1536, 1536], P('fsdp')
- key_weight_grad: float32 [1536, 512], P('fsdp')
- value_weight_grad: float32 [1536, 512], P('fsdp')
- output_weight_grad: float32 [1536, 1536], P('fsdp')
- router_weight_grad: float32 [1536, 20], P('fsdp')
- gate_weight_grad: float32 [20, 1536, 512], P('exp', 'fsdp')
- up_weight_grad: float32 [20, 1536, 512], P('exp', 'fsdp')
- down_weight_grad: float32 [20, 512, 1536], P('exp', 'fsdp')
The draws below stay inside these ranges and needn't reach their ends.
Inputs may be any that keep to these rules, and one draw needn't show every extreme that they name: `routes`: each row names 8 different experts. In the rows of one device no expert is named more than 128 times, a bound that some block reaches.
All inputs are finite; a program needn't handle non-finite values.
Results may differ from the reference program's by a relative error of at most 0.017.
Values may be sent and summed in bfloat16 or wider, within the bound.
No kernel may reach another device: no remote copies, remote signals or barrier semaphores. Data moves between devices by JAX's collectives and lax.ppermute only.
A program may use at most 192 MiB of HBM per device.

```python
import math
import jax
import jax.numpy as jnp
import numpy as np
from jax import lax

D = 1536
HEADS = 24
KV_HEADS = 8
HEAD = 64
FF = 512
TOP = 8
SEQ = 256
TOK_DEV = 256
EXPERTS = 20
TOKENS = 8192
SEQS = 32
CAP = 128


def set_ends(result, rng, low, high):
    shape = result.shape
    index_at = [jax.random.randint(jax.random.fold_in(rng, axis), (), 0, shape[axis]) for axis in range(len(shape))]
    result = result.at[tuple(index_at)].set(low)
    longest = shape.index(max(shape))
    index_at[longest] = (index_at[longest] + 1) % shape[longest]
    return result.at[tuple(index_at)].set(high)


def block_levels(stream_key, extent, split, smallest, top_value):
    level, own = 1.0, jax.random.fold_in(stream_key, 6)
    for dim, blocks in split:
        heights = jnp.exp(jax.random.uniform(jax.random.fold_in(own, dim), (blocks,), jnp.float32, smallest / len(split), top_value / len(split)))
        level = level * jnp.repeat(heights, extent[dim] // blocks).reshape([-1 if axis == dim else 1 for axis in range(len(extent))])
    return level


def shared_out(own_key, own, number, rows, amount, top, bound, slope):
    ranking = jax.random.permutation(own_key, amount)
    crowded, usual = load_shares(amount, rows * top, bound, slope, True), load_shares(amount, rows * top, bound, slope, False)
    places = jnp.arange(amount)

    def named(lengths, offset_by):
        used = int((lengths > 0).sum())
        fixed = max(1, used // 4)
        shifted = fixed + (places - fixed + offset_by * (used - fixed)) % max(1, amount - fixed)
        return jnp.zeros((amount,), jnp.int32).at[ranking[jnp.where(places < fixed, places, shifted)]].set(jnp.asarray(lengths, jnp.int32))

    lengths = jnp.where(number % 4 == 0, named(crowded, number // 4), named(usual, number - number // 4 - 1))
    mixed = jax.random.permutation(jax.random.fold_in(own, 3), amount)
    giver, sink = mixed[0:amount // 2 * 2:2], mixed[1:amount // 2 * 2:2]
    room = jnp.minimum(lengths[giver] - 1, bound - lengths[sink]) // 2
    room = jnp.where((giver == ranking[0]) | (sink == ranking[0]) | (lengths[sink] == 0), 0, jnp.maximum(room, 0))
    shifted = jax.random.randint(jax.random.fold_in(own, 4), (amount // 2,), 0, 1 << 20) % (room + 1)
    lengths = lengths.at[giver].add(-shifted).at[sink].add(shifted)
    labels = jnp.searchsorted(jnp.cumsum(lengths), jnp.arange(rows * top), side="right").astype(jnp.int32)
    table = labels.reshape(top, rows).T
    table = table[jax.random.permutation(jax.random.fold_in(own, 1), rows)]
    offset_by = jax.random.randint(jax.random.fold_in(own, 2), (rows, 1), 0, top)
    return jnp.take_along_axis(table, (jnp.arange(top)[None, :] + offset_by) % top, axis=1)


def load_shares(amount, total, bound, slope, full):
    weights = [(1 << 20) // math.isqrt(grade ** slope) + 1 for grade in range(1, amount + 1)]
    largest = bound if full else min(bound, max(-(-total // amount), total * weights[0] // sum(weights)))
    least = 1 if total - largest >= amount - 1 else 0
    counts, spare = [largest] + [least] * (amount - 1), total - largest - least * (amount - 1)
    while spare > 0:
        candidates = [i for i in range(1, amount) if counts[i] < largest] or [i for i in range(1, amount) if counts[i] < bound]
        whole, left = sum([weights[i] for i in candidates]), spare
        for i in candidates:
            more = min(bound - counts[i], max(1, left * weights[i] // whole), spare)
            counts[i] = counts[i] + more
            spare = spare - more
    return np.array(counts)


def scatter_about(rng, extent, width, bound, pieces=(), kind=jnp.bfloat16):
    drawn = width * jax.random.normal(rng, extent, jnp.float32)
    if pieces:
        drawn = drawn * block_levels(rng, extent, pieces, -0.22, 0.18)
    return jnp.clip(drawn, -bound, bound).astype(kind)


def setup_inputs(seed: int = 0) -> dict:
    streams_of = jax.random.split(jax.random.key(seed), 15)
    tokens = scatter_about(streams_of[0], (TOKENS, D), 1.0, 6.0, ((0, 32),))
    cotangent = scatter_about(streams_of[1], (TOKENS, D), 1.0, 6.0, ((0, 32),))
    prefix = set_ends(jax.random.randint(streams_of[2], (SEQS,), max(1, SEQ // 10), SEQ // 2 + 1), jax.random.fold_in(streams_of[2], 1), max(1, SEQ // 10), (SEQ // 2 + 1) - 1).astype(jnp.int32)
    routes_keys = jax.random.split(jax.random.fold_in(streams_of[3], 1), TOKENS // TOK_DEV)
    routes_turns = jax.random.permutation(jax.random.fold_in(streams_of[3], 3), TOKENS // TOK_DEV)
    routes = jax.vmap(lambda own, number: shared_out(jax.random.fold_in(streams_of[3], 2), own, number, TOK_DEV, EXPERTS, TOP, CAP, 2))(routes_keys, routes_turns).reshape((TOKENS, TOP))
    attention_gain = jnp.clip(1.0 + 0.1 * jax.random.normal(streams_of[4], (D,), jnp.float32), 0.5, 1.5).astype(jnp.bfloat16)
    expert_gain = jnp.clip(1.0 + 0.1 * jax.random.normal(streams_of[5], (D,), jnp.float32), 0.5, 1.5).astype(jnp.bfloat16)
    query_weight = scatter_about(streams_of[6], (D, D), (D // 2) ** -0.5, 0.21875, ((0, 8),))
    key_weight = scatter_about(streams_of[7], (D, KV_HEADS * HEAD), (D // 2) ** -0.5, 0.21875, ((0, 8),))
    value_weight = scatter_about(streams_of[8], (D, KV_HEADS * HEAD), D ** -0.5, 0.15625, ((0, 8),))
    output_weight = scatter_about(streams_of[9], (D, D), 0.3, 1.796875, ((0, 8),))
    router_weight = scatter_about(streams_of[10], (D, EXPERTS), (4 * D) ** -0.5, 0.078125, ((0, 8),))
    gate_weight = scatter_about(streams_of[11], (EXPERTS, D, FF), D ** -0.5, 0.15625, ((0, 4), (1, 8)))
    up_weight = scatter_about(streams_of[12], (EXPERTS, D, FF), D ** -0.5, 0.15625, ((0, 4), (1, 8)))
    down_weight = scatter_about(streams_of[13], (EXPERTS, FF, D), 0.7, 4.1875, ((0, 4), (1, 8)))
    return dict(tokens=tokens, cotangent=cotangent, prefix=prefix, routes=routes, attention_gain=attention_gain, expert_gain=expert_gain, query_weight=query_weight, key_weight=key_weight, value_weight=value_weight, output_weight=output_weight, router_weight=router_weight, gate_weight=gate_weight, up_weight=up_weight, down_weight=down_weight)


ATTENTION_SCALE = 0.015625
RESIDUAL_SCALE = 0.22
NORM_EPS = 1e-06
ROPE_BASE = 10000.0
MASKED = -1e+30

@jax.custom_vjp
def low(v):
    return lax.optimization_barrier(v.astype(jnp.bfloat16)).astype(jnp.float32)

@jax.custom_vjp
def low_back(v):
    return v

def low_keep(v):
    return (low(v), None)

def low_pass(kept, grad):
    return (grad,)

def back_keep(v):
    return (v, None)

def back_low(kept, grad):
    return (low(grad),)
low.defvjp(low_keep, low_pass)
low_back.defvjp(back_keep, back_low)

def product(left, right):
    return jnp.dot(left, right, precision=lax.Precision.HIGHEST, preferred_element_type=jnp.float32)

def rms_norm(values, gain):
    scale = lax.rsqrt(lax.optimization_barrier(jnp.mean(values * values, axis=-1, keepdims=True)) + NORM_EPS)
    return values * scale * gain

def rotary(length):
    half_width = HEAD // 2
    frequency = ROPE_BASE ** (-(jnp.arange(half_width).astype(jnp.float32) * (2.0 / HEAD)))
    angles = jnp.arange(length).astype(jnp.float32)[:, None] * frequency[None, :]
    return (jnp.cos(angles)[:, None, :], jnp.sin(angles)[:, None, :])

def rotate(values, cosine, sine_table):
    half_width = values.shape[-1] // 2
    first_half = values[..., :half_width]
    second_half = values[..., half_width:]
    return jnp.concatenate([first_half * cosine - second_half * sine_table, second_half * cosine + first_half * sine_table], axis=-1)

def attend_sequence(normed, prefix_len, query_weight, key_weight, value_weight, output_weight):
    length = normed.shape[0]
    group_size = HEADS // KV_HEADS
    cosine, sine_table = rotary(length)
    queries = low_back(product(normed, query_weight)).reshape(length, HEADS, HEAD)
    keys_raw = low_back(product(normed, key_weight)).reshape(length, KV_HEADS, HEAD)
    values = low(low_back(product(normed, value_weight))).reshape(length, KV_HEADS, HEAD)
    queries = low(rotate(queries, cosine, sine_table)).reshape(length, KV_HEADS, group_size, HEAD)
    keys_rot = low(rotate(keys_raw, cosine, sine_table))
    scores = jnp.einsum('qkgd,pkd->kgqp', queries, keys_rot, precision=lax.Precision.HIGHEST)
    scores = low_back(ATTENTION_SCALE * scores)
    positions = jnp.arange(length).astype(jnp.int32)
    visible = (positions[None, :] <= positions[:, None]) | (positions[None, :] < prefix_len.astype(jnp.int32))
    scores = jnp.where(visible, scores, MASKED)
    shares = low(jax.nn.softmax(scores, axis=-1))
    mixed_heads = jnp.einsum('kgqp,pkd->qkgd', shares, values, precision=lax.Precision.HIGHEST).reshape(length, HEADS * HEAD)
    mixed_heads = low(low_back(mixed_heads))
    return low_back(product(mixed_heads, output_weight))

def slot_positions(routes):
    flat_routes = routes.reshape(-1).astype(jnp.int32)
    expert_ids = jnp.arange(EXPERTS).astype(jnp.int32)
    onehot = (flat_routes[:, None] == expert_ids[None, :]).astype(jnp.int32)
    before = (jnp.cumsum(onehot, axis=0) - onehot).astype(jnp.int32)
    slot_index = lax.optimization_barrier(jnp.sum(before * onehot, axis=1)).astype(jnp.int32)
    return (flat_routes * CAP + slot_index).astype(jnp.int32)

def expert_block(normed, routes, router_weight, gate_weight, up_weight, down_weight):
    length = normed.shape[0]
    positions = slot_positions(routes)
    route_count = length * TOP
    sources = jnp.full((EXPERTS * CAP,), route_count, jnp.int32).at[positions].set(jnp.arange(route_count).astype(jnp.int32))
    token_index = (sources // TOP).astype(jnp.int32)
    padded = jnp.concatenate([normed, jnp.zeros((1, D), jnp.float32)], axis=0)
    token_rows = low_back(padded[token_index]).reshape(EXPERTS, CAP, D)
    gate_value = low_back(jnp.einsum('ecd,edf->ecf', token_rows, gate_weight, precision=lax.Precision.HIGHEST))
    up_value = low_back(jnp.einsum('ecd,edf->ecf', token_rows, up_weight, precision=lax.Precision.HIGHEST))
    hidden = low(jax.nn.silu(gate_value) * up_value)
    expert_out = low(low_back(jnp.einsum('ecf,efd->ecd', hidden, down_weight, precision=lax.Precision.HIGHEST)))
    picked = expert_out.reshape(EXPERTS * CAP, D)[positions].reshape(length, TOP, D)
    logits = low_back(product(normed, router_weight))
    chosen = jnp.take_along_axis(logits, routes.astype(jnp.int32), axis=1)
    gate_shares = jax.nn.softmax(chosen, axis=-1)
    return jnp.einsum('tk,tkd->td', gate_shares, picked, precision=lax.Precision.HIGHEST)

def block_forward(token_values, attention_gain, expert_gain, query_weight, key_weight, value_weight, output_weight, router_weight, gate_weight, up_weight, down_weight, prefix, routes):
    device_count = TOKENS // TOK_DEV
    dev_groups = math.gcd(device_count, max(1, 4096 // TOK_DEV))
    steps_count = device_count // dev_groups
    rows = dev_groups * TOK_DEV
    seqs_per = rows // SEQ
    grouped_tokens = token_values.reshape(steps_count, rows, D)
    grouped_prefix = prefix.reshape(steps_count, seqs_per)
    grouped_routes = routes.reshape(steps_count, dev_groups, TOK_DEV, TOP)

    def one_sequence(pair):
        return attend_sequence(pair[0], pair[1], query_weight, key_weight, value_weight, output_weight)

    def one_block(pair):
        return expert_block(pair[0], pair[1], router_weight, gate_weight, up_weight, down_weight)

    def group_step(triple):
        token_rows, prefix_rows, route_rows = triple
        normed = low(rms_norm(token_rows, attention_gain))
        attended = lax.map(jax.checkpoint(one_sequence), (normed.reshape(seqs_per, SEQ, D), prefix_rows)).reshape(rows, D)
        residual = token_rows + RESIDUAL_SCALE * attended
        normed_two = low(rms_norm(residual, expert_gain))
        mixture = lax.map(jax.checkpoint(one_block), (normed_two.reshape(dev_groups, TOK_DEV, D), route_rows)).reshape(rows, D)
        return residual + RESIDUAL_SCALE * mixture
    outputs = lax.map(jax.checkpoint(group_step), (grouped_tokens, grouped_prefix, grouped_routes))
    return outputs.reshape(TOKENS, D)

def reference(tokens, cotangent, prefix, routes, attention_gain, expert_gain, query_weight, key_weight, value_weight, output_weight, router_weight, gate_weight, up_weight, down_weight):
    floats = (tokens.astype(jnp.float32), attention_gain.astype(jnp.float32), expert_gain.astype(jnp.float32), query_weight.astype(jnp.float32), key_weight.astype(jnp.float32), value_weight.astype(jnp.float32), output_weight.astype(jnp.float32), router_weight.astype(jnp.float32), gate_weight.astype(jnp.float32), up_weight.astype(jnp.float32), down_weight.astype(jnp.float32))

    def forward(token_values, gain_one, gain_two, query_w, key_w, value_w, output_w, router_w, gate_w, up_w, down_w):
        return block_forward(token_values, gain_one, gain_two, query_w, key_w, value_w, output_w, router_w, gate_w, up_w, down_w, prefix, routes)
    output, pullback = jax.vjp(forward, *floats)
    gradients = pullback(cotangent.astype(jnp.float32))
    return (output.astype(jnp.bfloat16), gradients[0], gradients[1], gradients[2], gradients[3], gradients[4], gradients[5], gradients[6], gradients[7], gradients[8], gradients[9], gradients[10])
```

```python
import jax
import jax.numpy as jnp
from jax import lax
from jax.sharding import PartitionSpec as P

D = 1536
HEADS = 24
KV_HEADS = 8
HEAD = 64
TOP = 8
SEQ = 256
EXP_DEV = 5
CAP = 128
QKV = (HEADS + 2 * KV_HEADS) * HEAD
MISC = 128

ATTENTION_SCALE = 0.015625
RESIDUAL_SCALE = 0.22
NORM_EPS = 1e-06
ROPE_BASE = 10000.0
MASKED = -1e30

BF = jnp.bfloat16
F32 = jnp.float32


def rotary(length):
    half_width = HEAD // 2
    frequency = ROPE_BASE ** (-(jnp.arange(half_width).astype(jnp.float32) * (2.0 / HEAD)))
    angles = jnp.arange(length).astype(jnp.float32)[:, None] * frequency[None, :]
    return (jnp.cos(angles)[:, None, :], jnp.sin(angles)[:, None, :])


def rotate(values, cosine, sine_table):
    half_width = values.shape[-1] // 2
    first_half = values[..., :half_width]
    second_half = values[..., half_width:]
    return jnp.concatenate(
        [
            first_half * cosine - second_half * sine_table,
            second_half * cosine + first_half * sine_table,
        ],
        axis=-1,
    )


def unrotate(values, cosine, sine_table):
    half_width = values.shape[-1] // 2
    first_half = values[..., :half_width]
    second_half = values[..., half_width:]
    return jnp.concatenate(
        [
            first_half * cosine + second_half * sine_table,
            second_half * cosine - first_half * sine_table,
        ],
        axis=-1,
    )


def swap(values, bit):
    size = lax.axis_size("exp")
    return lax.ppermute(values, "exp", [(i, i ^ bit) for i in range(size)])


def gather_exp(values):
    far = swap(values, 2)
    near = swap(values, 1)
    both = swap(far, 1)
    return [values, near, far, both]


def scatter_exp(parts):
    near = swap(jnp.stack([parts[1].astype(BF), parts[3].astype(BF)]), 1)
    mine = parts[0] + near[0].astype(F32)
    other = (parts[2] + near[1].astype(F32)).astype(BF)
    return mine + swap(other, 2).astype(F32)


def ordered(blocks, me, axis):
    count = len(blocks)
    width = blocks[0].shape[axis]
    shape = list(blocks[0].shape)
    shape[axis] = width * count
    out = jnp.zeros(shape, blocks[0].dtype)
    for j, block in enumerate(blocks):
        out = lax.dynamic_update_slice_in_dim(out, block, (me ^ j) * width, axis)
    return out


def on_device(
    tokens,
    cotangent,
    prefix,
    routes,
    attention_gain,
    expert_gain,
    query_weight,
    key_weight,
    value_weight,
    output_weight,
    router_weight,
    gate_weight,
    up_weight,
    down_weight,
):
    owners = lax.axis_size("exp")
    shards = lax.axis_size("fsdp")
    me = lax.axis_index("exp")
    experts = EXP_DEV * owners
    length = tokens.shape[0]
    seq_count = length // SEQ
    group_size = HEADS // KV_HEADS
    group_width = group_size * HEAD
    piece = query_weight.shape[0] // owners

    def own_rows(weight):
        return lax.dynamic_slice_in_dim(weight, me * piece, piece, 0)

    misc = jnp.concatenate(
        [
            router_weight,
            attention_gain[:, None],
            expert_gain[:, None],
            jnp.zeros((router_weight.shape[0], MISC - experts - 2), BF),
        ],
        axis=1,
    )
    dense_piece = jnp.concatenate(
        [
            own_rows(w)
            for w in (query_weight, key_weight, value_weight, misc, output_weight)
        ],
        axis=1,
    )
    dense_quarter = lax.all_gather(dense_piece, "fsdp", axis=0, tiled=False)
    first_cols = QKV + MISC
    full_first = ordered(gather_exp(dense_quarter[:, :, :first_cols]), me, 1).reshape(D, first_cols)
    full_output = ordered(gather_exp(dense_quarter[:, :, first_cols:]), me, 1).reshape(D, D)
    full_qkv = full_first[:, :QKV]
    full_router = full_first[:, QKV : QKV + experts]
    gain_one = full_first[:, QKV + experts].astype(F32)
    gain_two = full_first[:, QKV + experts + 1].astype(F32)
    gate_full = lax.all_gather(gate_weight, "fsdp", axis=1, tiled=True)
    up_full = lax.all_gather(up_weight, "fsdp", axis=1, tiled=True)
    down_full = lax.all_gather(down_weight, "fsdp", axis=1, tiled=True)

    route_blocks = jnp.stack(gather_exp(routes))
    upstream_blocks = jnp.stack(gather_exp(cotangent))

    inputs = tokens.astype(F32)
    scale_one = lax.rsqrt(jnp.mean(inputs * inputs, axis=-1, keepdims=True) + NORM_EPS)
    normed_one = (inputs * scale_one * gain_one).astype(BF)
    projections = jnp.dot(normed_one, full_qkv, preferred_element_type=F32)
    queries = projections[:, : HEADS * HEAD]
    keys_raw = projections[:, HEADS * HEAD : (HEADS + KV_HEADS) * HEAD]
    values = projections[:, (HEADS + KV_HEADS) * HEAD :].astype(BF)
    cosine, sine_table = rotary(SEQ)
    queries_rot = (
        rotate(queries.reshape(seq_count, SEQ, HEADS, HEAD), cosine, sine_table)
        .astype(BF)
        .reshape(length, HEADS * HEAD)
    )
    keys_rot = (
        rotate(keys_raw.reshape(seq_count, SEQ, KV_HEADS, HEAD), cosine, sine_table)
        .astype(BF)
        .reshape(length, KV_HEADS * HEAD)
    )
    positions = jnp.arange(SEQ, dtype=jnp.int32)
    causal = positions[None, :] <= positions[:, None]
    visible = causal[None] | (positions[None, None, :] < prefix[:, None, None])
    visible_heads = visible[:, None]
    mixed_parts = []
    lse_parts = []
    for head_group in range(KV_HEADS):
        query_block = queries_rot[
            :, head_group * group_width : (head_group + 1) * group_width
        ].reshape(seq_count, SEQ, group_size, HEAD)
        key_block = keys_rot[:, head_group * HEAD : (head_group + 1) * HEAD].reshape(
            seq_count, SEQ, HEAD
        )
        value_block = values[:, head_group * HEAD : (head_group + 1) * HEAD].reshape(
            seq_count, SEQ, HEAD
        )
        scores = ATTENTION_SCALE * jnp.einsum(
            "bqgd,bpd->bgqp", query_block, key_block, preferred_element_type=F32
        )
        scores = jnp.where(visible_heads, scores, MASKED)
        highest = jnp.max(scores, axis=-1, keepdims=True)
        raised = jnp.exp(scores - highest)
        totals = jnp.sum(raised, axis=-1, keepdims=True)
        shares = (raised / totals).astype(BF)
        lse_parts.append(highest + jnp.log(totals))
        mixed_parts.append(
            jnp.einsum(
                "bgqp,bpd->bqgd", shares, value_block, preferred_element_type=F32
            ).reshape(length, group_width)
        )
    mixed_heads = jnp.concatenate(mixed_parts, axis=1).astype(BF)
    projected = jnp.dot(mixed_heads, full_output, preferred_element_type=F32)
    residual = inputs + RESIDUAL_SCALE * projected
    scale_two = lax.rsqrt(jnp.mean(residual * residual, axis=-1, keepdims=True) + NORM_EPS)
    normed_two = (residual * scale_two * gain_two).astype(BF)

    normed_blocks = jnp.stack(gather_exp(normed_two))
    logits = jnp.einsum("std,de->ste", normed_blocks, full_router, preferred_element_type=F32)
    expert_ids = jnp.arange(experts, dtype=jnp.int32)
    used = jnp.any(route_blocks[:, :, :, None] == expert_ids, axis=2)
    chosen = jnp.where(used, logits, MASKED)
    raised_gate = jnp.where(used, jnp.exp(chosen - jnp.max(chosen, axis=-1, keepdims=True)), 0.0)
    shares_all = raised_gate / jnp.sum(raised_gate, axis=-1, keepdims=True)
    used_here = lax.dynamic_slice_in_dim(used, me * EXP_DEV, EXP_DEV, 2)
    shares_here = lax.dynamic_slice_in_dim(shares_all, me * EXP_DEV, EXP_DEV, 2)
    block_rows = jnp.arange(length, dtype=jnp.int32)
    before = (block_rows[None, :] < block_rows[:, None]).astype(BF)
    slot = jnp.einsum("tr,sre->ste", before, used_here.astype(BF), preferred_element_type=F32)
    slot = jnp.where(used_here, slot.astype(jnp.int32), -1)
    slot_ids = jnp.arange(CAP, dtype=jnp.int32)
    hit = slot.transpose(2, 0, 1)[:, :, None, :] == slot_ids[None, None, :, None]
    select = hit.astype(BF)
    share_slot = jnp.sum(
        jnp.where(hit, shares_here.transpose(2, 0, 1)[:, :, None, :], 0.0), axis=-1
    )
    rows = owners * CAP
    arrived = (
        jnp.einsum("esct,std->escd", select, normed_blocks, preferred_element_type=F32)
        .astype(BF)
        .reshape(EXP_DEV, rows, D)
    )
    arrived_grads = (
        (
            jnp.einsum("esct,std->escd", select, upstream_blocks, preferred_element_type=F32)
            * (RESIDUAL_SCALE * share_slot[..., None])
        )
        .astype(BF)
        .reshape(EXP_DEV, rows, D)
    )
    gate_value = jnp.einsum("erd,edf->erf", arrived, gate_full, preferred_element_type=F32)
    up_value = jnp.einsum("erd,edf->erf", arrived, up_full, preferred_element_type=F32)
    gate_sigmoid = jax.nn.sigmoid(gate_value)
    activated = gate_value * gate_sigmoid
    hidden = (activated * up_value).astype(BF)
    weighted_out = (
        jnp.einsum("erf,efd->erd", hidden, down_full, preferred_element_type=F32)
        * share_slot.reshape(EXP_DEV, rows, 1)
    ).astype(BF)
    mixture_parts = jnp.einsum(
        "esct,escd->std",
        select,
        weighted_out.reshape(EXP_DEV, owners, CAP, D),
        preferred_element_type=F32,
    )
    mixture = scatter_exp([mixture_parts[j] for j in range(owners)])
    block_out = (residual + RESIDUAL_SCALE * mixture).astype(BF)

    hidden_grad = jnp.einsum(
        "erd,efd->erf", arrived_grads, down_full, preferred_element_type=F32
    )
    down_w_grad = jnp.einsum(
        "erf,erd->efd", hidden, arrived_grads, preferred_element_type=F32
    ).astype(BF)
    pull_slot = jnp.sum(hidden_grad * hidden.astype(F32), axis=-1).reshape(
        EXP_DEV, owners, CAP, 1
    )
    pull_here = jnp.sum(jnp.where(hit, pull_slot, 0.0), axis=2)
    pull = jnp.zeros((experts, length), F32)
    for j in range(owners):
        piece_j = pull_here[:, j]
        if j:
            piece_j = lax.ppermute(
                piece_j, "exp", [(i, i ^ j) for i in range(owners)]
            )
        pull = lax.dynamic_update_slice_in_dim(pull, piece_j, (me ^ j) * EXP_DEV, 0)
    pull = pull.T
    logit_grad = (pull - shares_all[0] * jnp.sum(pull, axis=-1, keepdims=True)).astype(BF)
    gate_pre_grad = (
        hidden_grad * up_value * gate_sigmoid * (1.0 + gate_value * (1.0 - gate_sigmoid))
    ).astype(BF)
    up_pre_grad = (hidden_grad * activated).astype(BF)
    gate_w_grad = jnp.einsum(
        "erd,erf->edf", arrived, gate_pre_grad, preferred_element_type=F32
    ).astype(BF)
    up_w_grad = jnp.einsum(
        "erd,erf->edf", arrived, up_pre_grad, preferred_element_type=F32
    ).astype(BF)
    row_grads = (
        jnp.einsum("erf,edf->erd", gate_pre_grad, gate_full, preferred_element_type=F32)
        + jnp.einsum("erf,edf->erd", up_pre_grad, up_full, preferred_element_type=F32)
    ).astype(BF)
    back_parts = jnp.einsum(
        "esct,escd->std",
        select,
        row_grads.reshape(EXP_DEV, owners, CAP, D),
        preferred_element_type=F32,
    )
    normed_two_grad = scatter_exp([back_parts[j] for j in range(owners)])
    down_sum = lax.psum_scatter(down_w_grad, "fsdp", scatter_dimension=1, tiled=True)
    gate_sum = lax.psum_scatter(gate_w_grad, "fsdp", scatter_dimension=1, tiled=True)
    up_sum = lax.psum_scatter(up_w_grad, "fsdp", scatter_dimension=1, tiled=True)

    upstream = cotangent.astype(F32)
    normed_two_grad = normed_two_grad + jnp.einsum(
        "te,de->td", logit_grad, full_router, preferred_element_type=F32
    )
    router_w_grad = jnp.einsum("td,te->de", normed_two, logit_grad, preferred_element_type=F32)
    inner_two = normed_two_grad * gain_two
    expert_gain_grad = jnp.sum(normed_two_grad * residual * scale_two, axis=0)
    cube_two = scale_two * scale_two * scale_two
    residual_grad = (
        upstream
        + scale_two * inner_two
        - residual * cube_two * jnp.mean(inner_two * residual, axis=-1, keepdims=True)
    )
    proj_grad = (RESIDUAL_SCALE * residual_grad).astype(BF)
    output_w_grad = jnp.einsum("tf,td->fd", mixed_heads, proj_grad, preferred_element_type=F32)
    mixed_grad = jnp.einsum(
        "td,fd->tf", proj_grad, full_output, preferred_element_type=F32
    ).astype(BF)
    query_parts = []
    key_parts = []
    value_parts = []
    for head_group in range(KV_HEADS):
        query_block = queries_rot[
            :, head_group * group_width : (head_group + 1) * group_width
        ].reshape(seq_count, SEQ, group_size, HEAD)
        key_block = keys_rot[:, head_group * HEAD : (head_group + 1) * HEAD].reshape(
            seq_count, SEQ, HEAD
        )
        value_block = values[:, head_group * HEAD : (head_group + 1) * HEAD].reshape(
            seq_count, SEQ, HEAD
        )
        grad_block = mixed_grad[
            :, head_group * group_width : (head_group + 1) * group_width
        ].reshape(seq_count, SEQ, group_size, HEAD)
        scores = ATTENTION_SCALE * jnp.einsum(
            "bqgd,bpd->bgqp", query_block, key_block, preferred_element_type=F32
        )
        scores = jnp.where(visible_heads, scores, MASKED)
        shares_float = jnp.exp(scores - lse_parts[head_group])
        shares = shares_float.astype(BF)
        share_grad = jnp.einsum(
            "bqgd,bpd->bgqp", grad_block, value_block, preferred_element_type=F32
        )
        row_delta = jnp.sum(shares_float * share_grad, axis=-1, keepdims=True)
        score_grad = (shares_float * (share_grad - row_delta)).astype(BF)
        query_parts.append(
            ATTENTION_SCALE
            * jnp.einsum(
                "bgqp,bpd->bqgd", score_grad, key_block, preferred_element_type=F32
            ).reshape(length, group_width)
        )
        key_parts.append(
            ATTENTION_SCALE
            * jnp.einsum(
                "bgqp,bqgd->bpd", score_grad, query_block, preferred_element_type=F32
            ).reshape(length, HEAD)
        )
        value_parts.append(
            jnp.einsum(
                "bgqp,bqgd->bpd", shares, grad_block, preferred_element_type=F32
            ).reshape(length, HEAD)
        )
    query_grad = (
        unrotate(
            jnp.concatenate(query_parts, axis=1).reshape(seq_count, SEQ, HEADS, HEAD),
            cosine,
            sine_table,
        )
        .reshape(length, HEADS * HEAD)
        .astype(BF)
    )
    key_grad = (
        unrotate(
            jnp.concatenate(key_parts, axis=1).reshape(seq_count, SEQ, KV_HEADS, HEAD),
            cosine,
            sine_table,
        )
        .reshape(length, KV_HEADS * HEAD)
        .astype(BF)
    )
    value_grad = jnp.concatenate(value_parts, axis=1).astype(BF)
    qkv_grad = jnp.concatenate([query_grad, key_grad, value_grad], axis=1)
    qkv_w_grad = jnp.einsum("td,tf->df", normed_one, qkv_grad, preferred_element_type=F32)
    normed_one_grad = jnp.einsum("tf,df->td", qkv_grad, full_qkv, preferred_element_type=F32)
    inner_one = normed_one_grad * gain_one
    attention_gain_grad = jnp.sum(normed_one_grad * inputs * scale_one, axis=0)
    cube_one = scale_one * scale_one * scale_one
    input_grad = (
        residual_grad
        + scale_one * inner_one
        - inputs * cube_one * jnp.mean(inner_one * inputs, axis=-1, keepdims=True)
    )

    def piece_sum(grad):
        shaped = grad.reshape(shards, owners * piece, grad.shape[1])
        return scatter_exp(
            [
                lax.dynamic_slice_in_dim(shaped, (me ^ j) * piece, piece, 1)
                for j in range(owners)
            ]
        ).astype(BF)

    misc_grad = jnp.concatenate(
        [
            router_w_grad,
            attention_gain_grad[:, None],
            expert_gain_grad[:, None],
            jnp.zeros((D, MISC - experts - 2), F32),
        ],
        axis=1,
    )
    dense_sums = jnp.concatenate(
        [piece_sum(qkv_w_grad), piece_sum(misc_grad), piece_sum(output_w_grad)], axis=2
    )
    dense_part = lax.psum_scatter(dense_sums, "fsdp", scatter_dimension=0, tiled=True)
    dense_sum = ordered(gather_exp(dense_part[0]), me, 0).astype(F32)
    edges = [HEADS * HEAD, (HEADS + KV_HEADS) * HEAD, QKV, first_cols]
    query_sum, key_sum, value_sum, misc_sum, output_sum = jnp.split(dense_sum, edges, axis=1)
    return (
        block_out,
        input_grad,
        misc_sum[:, experts],
        misc_sum[:, experts + 1],
        query_sum,
        key_sum,
        value_sum,
        output_sum,
        misc_sum[:, :experts],
        gate_sum.astype(F32),
        up_sum.astype(F32),
        down_sum.astype(F32),
    )


def solution(mesh):
    in_specs = (
        P(("exp", "fsdp"), None),
        P(("exp", "fsdp"), None),
        P(("exp", "fsdp")),
        P(("exp", "fsdp"), None),
        P("fsdp"),
        P("fsdp"),
        P("fsdp", None),
        P("fsdp", None),
        P("fsdp", None),
        P("fsdp", None),
        P("fsdp", None),
        P("exp", "fsdp", None),
        P("exp", "fsdp", None),
        P("exp", "fsdp", None),
    )
    out_specs = (
        P(("exp", "fsdp"), None),
        P(("exp", "fsdp"), None),
        P("fsdp"),
        P("fsdp"),
        P("fsdp", None),
        P("fsdp", None),
        P("fsdp", None),
        P("fsdp", None),
        P("fsdp", None),
        P("exp", "fsdp", None),
        P("exp", "fsdp", None),
        P("exp", "fsdp", None),
    )
    return jax.shard_map(
        on_device, mesh=mesh, in_specs=in_specs, out_specs=out_specs, check_vma=False
    )
```
